32 devices in a mesh: gx: 4 (over y, x), gy: 4 (over z), gz: 2 (over core).
Axes of the slice: x: 2, y: 2, z: 4, core: 2. Of those that a mesh axis runs over, the one named last changes fastest.
Arguments:
- positions: float32 [2048, 3, 128], P(('gx', 'gy', 'gz')), may hold values from 0 to 1
- charges: float32 [2048, 128], P(('gx', 'gy', 'gz')), may hold values from -0.18 to 0.18
- counts: int32 [2048], P(('gx', 'gy', 'gz')), may hold values from 1 to 128
- up_inverse: float32 [64, 64], replicated, may hold values from -0.09375 to 0.09375
- down_inverse: float32 [64, 64], replicated, may hold values from -0.09375 to 0.09375
- inner_surface: float32 [3, 64], replicated, may hold values from 0.15 to 0.85
- outer_surface: float32 [3, 64], replicated, may hold values from -1 to 2, as said below
Outputs:
- potential: float32 [2048, 128], P(('gx', 'gy', 'gz'))
The draws below stay inside these ranges and needn't reach their ends.
Inputs may be any that keep to these rules, and one draw needn't show every extreme that they name: `outer_surface`: each point lies on the boundary of the cube [-1, 2]^3.
All inputs are finite; a program needn't handle non-finite values.
Results may differ from the reference program's by a relative error of at most 0.0003.
Values sent between devices are 32-bit elements; how exact they have to be, the bound alone decides.
A program may use at most 64 MiB of HBM per device.

```python
from functools import partial
import jax
import jax.numpy as jnp
import numpy as np
from jax import lax

CX = 4
CY = 4
CZ = 4
PTS = 128
TERMS = 64
LEAVES = 2048
DEVICES = 32


def draw_outer_surface(key, part):
    first_key, second_key, third_key = jax.random.split(jax.random.fold_in(key, 7), 3)
    spot = jax.random.uniform(first_key, (3, TERMS), jnp.float32, -1.0, 1.0)
    facing = jax.random.randint(second_key, (TERMS,), 0, 3)
    signed = jax.random.randint(third_key, (TERMS,), 0, 2).astype(jnp.float32) * 2.0 - 1.0
    picked = jnp.arange(3)[:, None] == facing[None, :]
    cube = jnp.where(picked, signed[None, :], spot)
    return 0.5 + 1.5 * cube


def set_ends(array, key, least, top_value):
    dims = array.shape
    place = [jax.random.randint(jax.random.fold_in(key, axis), (), 0, dims[axis]) for axis in range(len(dims))]
    array = array.at[tuple(place)].set(least)
    longest = dims.index(max(dims))
    place[longest] = (place[longest] + 1) % dims[longest]
    return array.at[tuple(place)].set(top_value)


def shard_levels(rng, shape, pieces, low, high):
    gain = 1.0
    for axis_at, blocks in pieces:
        heights = jax.random.uniform(jax.random.fold_in(jax.random.fold_in(rng, 6), axis_at), (blocks,), jnp.float32, low / len(pieces), high / len(pieces))
        gain = gain * jnp.repeat(jnp.exp(heights), shape[axis_at] // blocks).reshape((-1,) + (1,) * (len(shape) - 1 - axis_at))
    return gain


def noise(own_key, shape, scale, limit, cuts=(), kind=jnp.bfloat16):
    drawn = jax.random.normal(own_key, shape, jnp.float32) * scale
    if len(cuts) > 0:
        drawn = shard_levels(own_key, shape, cuts, -0.22, 0.18) * drawn
    return jnp.clip(drawn, min=-limit, max=limit).astype(kind)


def setup_inputs(seed: int = 0) -> dict:
    key_list = jax.random.split(jax.random.key(seed), 8)
    return {
        "positions": jnp.clip(1.0 * jax.random.uniform(key_list[0], (LEAVES, 3, PTS), jnp.float32) ** shard_levels(key_list[0], (LEAVES, 3, PTS), ((0, 32),), -0.2, 0.2), 0.0, 1.0),
        "charges": noise(key_list[1], (LEAVES, PTS), 0.03, 0.18, ((0, 32),), jnp.float32),
        "counts": set_ends(jax.random.randint(key_list[2], (LEAVES,), 1, PTS + 1), jax.random.fold_in(key_list[2], 1), 1, PTS).astype(jnp.int32),
        "up_inverse": noise(key_list[3], (TERMS, TERMS), (TERMS * TERMS) ** -0.5, 0.09375, (), jnp.float32),
        "down_inverse": noise(key_list[4], (TERMS, TERMS), (TERMS * TERMS) ** -0.5, 0.09375, (), jnp.float32),
        "inner_surface": jnp.clip(jax.random.uniform(key_list[5], (3, TERMS), jnp.float32, 0.15, 0.85), 0.15, 0.85),
        "outer_surface": draw_outer_surface(jax.random.fold_in(key_list[7], 71), 0),
    }


SOFTEN = 0.0025
EXACT_DOTS = lax.Precision.HIGHEST

def kernel(square):
    return 1.0 / jnp.sqrt(square + SOFTEN)

def leaf_blocks(function, arrays, block_size):
    leaf_count = arrays[0].shape[0]
    shaped = tuple((member.reshape((leaf_count // block_size, block_size) + member.shape[1:]) for member in arrays))
    result = lax.map(lambda members: function(*members), shaped)
    return result.reshape((leaf_count,) + result.shape[2:])

def upward(outer, position, charge):
    square = jnp.zeros((position.shape[0], outer.shape[1], position.shape[2]), jnp.float32)
    for dimension in range(3):
        spread = outer[dimension][None, :, None] - position[:, dimension, None, :]
        square = square + spread * spread
    return jnp.einsum('nij,nj->ni', kernel(square), charge, precision=EXACT_DOTS)

def downward(outer, position, weight):
    square = jnp.zeros((position.shape[0], position.shape[2], outer.shape[1]), jnp.float32)
    for dimension in range(3):
        spread = position[:, dimension, :, None] - outer[dimension][None, None, :]
        square = square + spread * spread
    return jnp.einsum('nti,ni->nt', kernel(square), weight, precision=EXACT_DOTS)

def pair_potential(target, source, shift, exclude):
    square = jnp.zeros((target.shape[0], target.shape[2], source.shape[2]), jnp.float32)
    for dimension in range(3):
        spread = target[:, dimension, :, None] - source[:, dimension, None, :] - shift[dimension]
        square = square + spread * spread
    weight = kernel(square)
    if exclude:
        weight = weight * (1.0 - jnp.eye(target.shape[2], dtype=jnp.float32))
    return jnp.einsum('nts,ns->nt', weight, source[:, 3, :], precision=EXACT_DOTS)

def allowed(parity, shift):
    return jnp.abs(jnp.floor_divide(parity + shift, 2)) <= 1

def translate(extended, inner, span_x, span_y, span_z):
    parity_x = jnp.arange(span_x, dtype=jnp.int32) % 2
    parity_y = jnp.arange(span_y, dtype=jnp.int32) % 2
    parity_z = jnp.arange(span_z, dtype=jnp.int32) % 2
    shifts_z = jnp.arange(-3, 4, dtype=jnp.int32)
    terms_count = inner.shape[1]

    def over_x(accum, shift_x):
        slab = lax.dynamic_slice_in_dim(extended, shift_x + 3, span_x, axis=0)
        okay_x = allowed(parity_x, shift_x)
        okay_z = allowed(parity_z[None, :], shifts_z[:, None])
        spread_x = inner[0][:, None] - inner[0][None, :] - shift_x.astype(jnp.float32)
        spread_z = inner[2][None, :, None] - inner[2][None, None, :] - shifts_z.astype(jnp.float32)[:, None, None]
        for shift_y in range(-3, 4):
            rows = slab[:, 3 + shift_y:3 + shift_y + span_y]
            stacked = jnp.stack([rows[:, :, 3 + shift_z:3 + shift_z + span_z] for shift_z in range(-3, 4)])
            okay_y = allowed(parity_y, shift_y)
            spread_y = inner[1][:, None] - inner[1][None, :] - float(shift_y)
            square = (spread_x * spread_x + spread_y * spread_y)[None] + spread_z * spread_z
            matrices = kernel(square)
            extent = jnp.maximum(jnp.maximum(jnp.abs(shift_x), abs(shift_y)), jnp.abs(shifts_z))
            mask = okay_x[None, :, None, None] & okay_y[None, None, :, None] & okay_z[:, None, None, :] & (extent >= 2)[:, None, None, None]
            weighted = stacked * mask[..., None].astype(jnp.float32)
            accum = accum + jnp.einsum('oxyzj,oij->xyzi', weighted, matrices, precision=EXACT_DOTS)
        return (accum, None)
    start = jnp.zeros((span_x, span_y, span_z, terms_count), jnp.float32)
    result, _ = lax.scan(over_x, start, jnp.arange(-3, 4, dtype=jnp.int32))
    return result

def box_tables():
    total_bits = DEVICES.bit_length() - 1
    bit_counts = [len(range(dimension, total_bits, 3)) for dimension in range(3)]
    corners = np.zeros((DEVICES, 3), np.int32)
    for device in range(DEVICES):
        for dimension in range(3):
            corners[device, dimension] = sum(((device >> dimension + 3 * rank & 1) << rank for rank in range(bit_counts[dimension])))
    extent = [1 << bit_counts[dimension] for dimension in range(3)]
    device_table = np.zeros(extent, np.int32)
    device_table[corners[:, 0], corners[:, 1], corners[:, 2]] = np.arange(DEVICES, dtype=np.int32)
    return (corners, device_table, extent)

def to_grid(flat, device_table, extent):
    trailing = flat.shape[1:]
    blocks = flat.reshape((DEVICES, CX, CY, CZ) + trailing)[device_table]
    permuted = (0, 3, 1, 4, 2, 5) + tuple(range(6, 6 + len(trailing)))
    return blocks.transpose(permuted).reshape((extent[0] * CX, extent[1] * CY, extent[2] * CZ) + trailing)

def from_grid(grid, corners, extent):
    trailing = grid.shape[3:]
    shaped = grid.reshape((extent[0], CX, extent[1], CY, extent[2], CZ) + trailing)
    permuted = (0, 2, 4, 1, 3, 5) + tuple(range(6, 6 + len(trailing)))
    shaped = shaped.transpose(permuted)
    blocks = shaped[corners[:, 0], corners[:, 1], corners[:, 2]]
    return blocks.reshape((DEVICES * CX * CY * CZ,) + trailing)

def reference(positions, charges, counts, up_inverse, down_inverse, inner_surface, outer_surface):
    live = (jnp.arange(PTS, dtype=jnp.int32)[None, :] < counts[:, None]).astype(jnp.float32)
    source = charges * live
    check_up = leaf_blocks(partial(upward, outer_surface), (positions, source), 64)
    density = jnp.dot(check_up, up_inverse.T, preferred_element_type=jnp.float32, precision=EXACT_DOTS)
    corners, device_table, extent = box_tables()
    grid_x, grid_y, grid_z = (extent[0] * CX, extent[1] * CY, extent[2] * CZ)
    cell_total = grid_x * grid_y * grid_z
    dens_grid = to_grid(density, device_table, extent)
    point_grid = to_grid(jnp.concatenate([positions, source[:, None, :]], axis=1), device_table, extent)
    targets = point_grid[:, :, :, :3].reshape(cell_total, 3, PTS)
    padded = jnp.pad(point_grid, ((1, 1), (1, 1), (1, 1), (0, 0), (0, 0)))
    near = jnp.zeros((cell_total, PTS), jnp.float32)
    for shift_x in range(-1, 2):
        for shift_y in range(-1, 2):
            for shift_z in range(-1, 2):
                window = padded[1 + shift_x:1 + shift_x + grid_x, 1 + shift_y:1 + shift_y + grid_y, 1 + shift_z:1 + shift_z + grid_z]
                window = window.reshape(cell_total, 4, PTS)
                exclude = shift_x == 0 and shift_y == 0 and (shift_z == 0)
                near = near + leaf_blocks(partial(pair_potential, shift=(shift_x, shift_y, shift_z), exclude=exclude), (targets, window), 64)
    near = from_grid(near.reshape(grid_x, grid_y, grid_z, PTS), corners, extent)
    extended = jnp.pad(dens_grid, ((3, 3), (3, 3), (3, 3), (0, 0)))
    check_down = translate(extended, inner_surface, grid_x, grid_y, grid_z)
    check_down = from_grid(check_down, corners, extent)
    local = jnp.dot(check_down, down_inverse.T, preferred_element_type=jnp.float32, precision=EXACT_DOTS)
    far = leaf_blocks(partial(downward, outer_surface), (positions, local), 64)
    return live * (near + far)
```

```python
from functools import partial

import jax
import jax.numpy as jnp
from jax import lax
from jax.experimental import pallas as pl
from jax.experimental.pallas import tpu as pltpu
from jax.sharding import PartitionSpec as P

CX = 4
CY = 4
CZ = 4
PTS = 128
TERMS = 64
LEAF = CX * CY * CZ
EXT = (CX + 2) * (CY + 2) * (CZ + 2)
FEATS = 32


SOFTEN = 0.0025
EXACT_DOTS = lax.Precision.HIGHEST


def from_partner(value, axis, stride):
    mask = 2**stride
    pairs = [(source, source ^ mask) for source in range(lax.axis_size(axis))]
    return lax.ppermute(value, axis, pairs)


def iota(shape, dimension):
    return lax.broadcasted_iota(jnp.int32, shape, dimension)


def column(row):
    size = row.shape[1]
    eye = iota((size, size), 0) == iota((size, size), 1)
    return jnp.sum(jnp.where(eye, row, 0.0), axis=1, keepdims=True)


def rounded(value):
    return value.astype(jnp.bfloat16).astype(jnp.float32)


def three_parts(value):
    high = rounded(value)
    middle = rounded(value - high)
    low = rounded(value - high - middle)
    return high, middle, low


def upward_body(pos_ref, charge_ref, count_ref, up_ref, outer_ref, points_ref, dens_ref):
    lane = iota((1, PTS), 1)
    lanes = iota((TERMS, PTS), 1)
    spots = [jnp.broadcast_to(column(outer_ref[c : c + 1, :]), (TERMS, PTS)) for c in range(3)]

    def leaf(n, check):
        place = pos_ref[n]
        source = jnp.where(lane < count_ref[n], charge_ref[pl.ds(n, 1), :], 0.0)
        points_ref[n] = jnp.concatenate([place, source], axis=0)
        square = jnp.full((TERMS, PTS), SOFTEN, jnp.float32)
        for c in range(3):
            spread = spots[c] - place[c : c + 1, :]
            square = square + spread * spread
        total = jnp.sum(lax.rsqrt(square) * source, axis=1, keepdims=True)
        return jnp.where(lanes == n, total, check)

    check = lax.fori_loop(0, LEAF, leaf, jnp.zeros((TERMS, PTS), jnp.float32), unroll=4)
    dens = jnp.dot(
        up_ref[...], check, preferred_element_type=jnp.float32, precision=EXACT_DOTS
    )
    dens_ref[...] = jnp.transpose(dens)[:LEAF]


def squares_of(points, shift_x, shift_y, shift_z, extra):
    row = iota((8, PTS), 0) % 4
    twice = jnp.concatenate([points, points], axis=0)
    place = twice + jnp.where(row == 0, shift_x, jnp.where(row == 1, shift_y, shift_z))
    square = place * place
    norm = square[0:1] + square[1:2] + square[2:3] + extra
    return jnp.where(row == 3, norm, place), row == 3, iota((8, PTS), 0) < 4


def source_features(points, shift_x, shift_y, shift_z):
    value, last, first = squares_of(points, shift_x, shift_y, shift_z, 0.0)
    high, middle, low = three_parts(value)
    scale = jnp.where(last, 1.0, -2.0)
    high_one = jnp.where(last, 1.0, -2.0 * high)
    middle_one = jnp.where(last, 1.0, -2.0 * middle)
    rows = [
        jnp.where(first, high * scale, middle * scale),
        jnp.where(first, low * scale, high_one),
        jnp.where(first, high_one, middle_one),
        jnp.zeros((8, PTS), jnp.float32),
    ]
    return jnp.concatenate(rows, axis=0).astype(jnp.bfloat16)


def target_features(points, shift_x, shift_y, shift_z):
    value, last, first = squares_of(points, shift_x, shift_y, shift_z, SOFTEN)
    high, middle, low = three_parts(value)
    high_one = jnp.where(last, 1.0, high)
    rows = [
        high_one,
        jnp.where(first, high_one, jnp.where(last, high, middle)),
        jnp.where(first, jnp.where(last, middle, low), jnp.where(last, low, middle)),
        jnp.zeros((8, PTS), jnp.float32),
    ]
    return jnp.transpose(jnp.concatenate(rows, axis=0)).astype(jnp.bfloat16)


def translate_part(dens_ref, inner_ref, down_ref, wide, grouped, local):
    dens = dens_ref[...]
    high = rounded(dens)
    wide[...] = jnp.concatenate([high, rounded(dens - high)], axis=1)

    def clear(n, carry):
        grouped[pl.ds(n * 8, 8)] = jnp.zeros((8, 8, 2 * TERMS), jnp.float32)
        return carry

    lax.fori_loop(0, 64, clear, 0)

    def gather(n, carry):
        a_x = n // 6
        a_y = n % 6
        for a_z in range(6):
            to = (a_x + 1) * 64 + (a_y + 1) * 8 + a_z + 1
            for parent in range(8):
                cell_x = 2 * (parent // 4) + a_x
                cell_y = 2 * (parent // 2 % 2) + a_y
                cell_z = 2 * (parent % 2) + a_z
                cell = cell_x * 64 + cell_y * 8 + cell_z
                grouped[to, parent : parent + 1, :] = wide[pl.ds(cell, 1), :]
        return carry

    lax.fori_loop(0, 36, gather, 0)

    first = iota((TERMS, 2 * TERMS), 1) < TERMS
    spread = []
    for c in range(3):
        row = inner_ref[c : c + 1, :]
        spread.append(jnp.concatenate([row, row], axis=1) - column(row))

    def shift_pair(n, total):
        shift_x = n // 7 - 3
        shift_y = n % 7 - 3
        d_x = spread[0] - shift_x.astype(jnp.float32)
        d_y = spread[1] - shift_y.astype(jnp.float32)
        plane = d_x * d_x + d_y * d_y + SOFTEN
        extent = jnp.maximum(jnp.abs(shift_x), jnp.abs(shift_y))
        lefts = []
        rights = []
        for shift_z in range(-3, 4):
            d_z = spread[2] - float(shift_z)
            weight = lax.rsqrt(plane + d_z * d_z)
            if abs(shift_z) < 2:
                weight = jnp.where(extent >= 2, weight, 0.0)
            upper = rounded(weight)
            right = jnp.where(first, upper, weight - upper).astype(jnp.bfloat16)
            rights += [right, right]
            pieces = []
            for parity in range(8):
                at = (
                    (shift_x + 3 + parity // 4) * 64
                    + (shift_y + 3 + parity // 2 % 2) * 8
                    + shift_z + 3 + parity % 2
                )
                pieces.append(grouped[at])
            lefts.append(jnp.concatenate(pieces, axis=0).astype(jnp.bfloat16))
        for at in range(0, 7, 2):
            left = jnp.concatenate(lefts[at : at + 2], axis=1)
            right = jnp.concatenate(rights[2 * at : 2 * at + 4], axis=0)
            total = total + jnp.dot(left, right, preferred_element_type=jnp.float32)
        return total

    total = lax.fori_loop(0, 49, shift_pair, jnp.zeros((LEAF, 2 * TERMS), jnp.float32))
    down = down_ref[...]
    down = jnp.concatenate([down, down], axis=1)
    down = jnp.concatenate([down, jnp.zeros_like(down)], axis=0)
    local[...] = lax.dot_general(
        total,
        down,
        (((1,), (1,)), ((), ())),
        preferred_element_type=jnp.float32,
        precision=EXACT_DOTS,
    )


def near_body(
    count_ref,
    points_ref,
    dens_ref,
    down_ref,
    inner_ref,
    outer_ref,
    out_ref,
    wide,
    grouped,
    local,
    sources,
    targets,
    surface,
):
    translate_part(dens_ref, inner_ref, down_ref, wide, grouped, local)
    surface[...] = jnp.zeros((4, PTS), jnp.float32)
    surface[0:3, 0:TERMS] = outer_ref[...]

    def middle(cell):
        return cell.astype(jnp.float32) - (CX // 2 + 1)

    def prepare(n, carry):
        e_x = n // ((CY + 2) * (CZ + 2))
        e_y = n // (CZ + 2) % (CY + 2)
        e_z = n % (CZ + 2)
        sources[n] = source_features(points_ref[n], middle(e_x), middle(e_y), middle(e_z))
        return carry

    lax.fori_loop(0, EXT, prepare, 0, unroll=4)

    def ext_index(n):
        return (n // (CY * CZ) + 1) * ((CY + 2) * (CZ + 2)) + (n // CZ % CY + 1) * (CZ + 2) + (
            n % CZ + 1
        )

    def prepare_own(n, carry):
        x = middle(n // (CY * CZ) + 1)
        y = middle(n // CZ % CY + 1)
        z = middle(n % CZ + 1)
        targets[n] = target_features(points_ref[ext_index(n)], x, y, z)
        sources[EXT + n] = source_features(surface[...], x, y, z)
        return carry

    lax.fori_loop(0, LEAF, prepare_own, 0, unroll=4)

    lane = iota((1, PTS), 1)

    def leaf(n, carry):
        base = ext_index(n)
        x = n // (CY * CZ)
        y = n // CZ % CY
        z = n % CZ
        parity = (x % 2) * 4 + (y % 2) * 2 + z % 2
        parent = (x // 2) * 4 + (y // 2) * 2 + z // 2
        count = count_ref[n]
        blocks = []
        for s_x in range(-1, 2):
            for s_y in range(-1, 2):
                for s_z in range(-1, 2):
                    blocks.append(base + s_x * ((CY + 2) * (CZ + 2)) + s_y * (CZ + 2) + s_z)

        def rows(size):
            left = targets[n, 0:size, :]
            eye = iota((size, PTS), 0) == iota((size, PTS), 1)
            total = jnp.zeros((size, PTS), jnp.float32)
            for at in range(0, 28, 2):
                right = []
                charge = []
                for b in (at, at + 1):
                    if b < 27:
                        right.append(sources[blocks[b]])
                        charge.append(points_ref[blocks[b], 3:4, :])
                    else:
                        right.append(sources[EXT + n])
                        charge.append(local[pl.ds(parity * 8 + parent, 1), :])
                square = jnp.dot(
                    left, jnp.concatenate(right, axis=1), preferred_element_type=jnp.float32
                )
                weight = lax.rsqrt(square)
                for k, b in enumerate((at, at + 1)):
                    part = weight[:, k * PTS : (k + 1) * PTS]
                    if b == 13:
                        part = jnp.where(eye, 0.0, part)
                    total = total + part * charge[k]
            sums = jnp.sum(total, axis=1, keepdims=True)
            flat = jnp.sum(jnp.where(eye, sums, 0.0), axis=0, keepdims=True)
            out_ref[pl.ds(n, 1), :] = jnp.where(lane < count, flat, 0.0)

        filled = (count + 31) // 32
        for k in range(1, 5):
            pl.when(filled == k)(partial(rows, 32 * k))
        return carry

    lax.fori_loop(0, LEAF, leaf, 0)


def whole():
    return pl.BlockSpec(memory_space=pltpu.VMEM)


def scalars():
    return pl.BlockSpec(memory_space=pltpu.SMEM)


def upward(positions, charges, counts, up_inverse, outer_surface):
    return pl.pallas_call(
        upward_body,
        out_shape=(
            jax.ShapeDtypeStruct((LEAF, 4, PTS), jnp.float32),
            jax.ShapeDtypeStruct((LEAF, TERMS), jnp.float32),
        ),
        in_specs=[whole(), whole(), scalars(), whole(), whole()],
        out_specs=(whole(), whole()),
        name="upward",
    )(positions, charges, counts, up_inverse, outer_surface)


def potentials(counts, points, density, down_inverse, inner_surface, outer_surface):
    return pl.pallas_call(
        near_body,
        out_shape=jax.ShapeDtypeStruct((LEAF, PTS), jnp.float32),
        in_specs=[scalars()] + [whole()] * 5,
        out_specs=whole(),
        scratch_shapes=[
            pltpu.VMEM((512, 2 * TERMS), jnp.float32),
            pltpu.VMEM((512, 8, 2 * TERMS), jnp.float32),
            pltpu.VMEM((LEAF, 2 * TERMS), jnp.float32),
            pltpu.VMEM((EXT + LEAF, FEATS, PTS), jnp.bfloat16),
            pltpu.VMEM((LEAF, PTS, FEATS), jnp.bfloat16),
            pltpu.VMEM((4, PTS), jnp.float32),
        ],
        compiler_params=pltpu.CompilerParams(vmem_limit_bytes=50 * 2**20),
        name="potentials",
    )(counts, points, density, down_inverse, inner_surface, outer_surface)


def axis_bits():
    low_bits = lax.axis_size("gz").bit_length() - 1
    mid_bits = lax.axis_size("gy").bit_length() - 1
    high_bits = lax.axis_size("gx").bit_length() - 1
    return (low_bits, mid_bits, high_bits)


def flip(rising_dens, rising_points, falling_dens, falling_points, global_bit):
    low_bits, mid_bits, high_bits = axis_bits()
    if global_bit < low_bits:
        return from_partner(
            (rising_dens, rising_points, falling_dens, falling_points), "gz", global_bit
        )
    if global_bit < low_bits + mid_bits:
        return from_partner(
            (rising_dens, rising_points, falling_dens, falling_points), "gy", global_bit - low_bits
        )
    return from_partner(
        (rising_dens, rising_points, falling_dens, falling_points),
        "gx",
        global_bit - low_bits - mid_bits,
    )


def box_place(device, dimension, total_bits):
    place = jnp.zeros((), jnp.int32)
    for bit_rank, global_bit in enumerate(range(dimension, total_bits, 3)):
        place = place + jnp.left_shift(
            jnp.bitwise_and(jnp.right_shift(device, global_bit), 1), bit_rank
        )
    return place


def extend(density, points, dimension, layers, device, total_bits):
    position = box_place(device, dimension, total_bits)
    dens_size = density.shape[dimension]
    point_size = points.shape[dimension]
    rising_dens = lax.slice_in_dim(density, dens_size - layers, dens_size, axis=dimension)
    rising_points = lax.slice_in_dim(points, point_size - 1, point_size, axis=dimension)
    falling_dens = lax.slice_in_dim(density, 0, layers, axis=dimension)
    falling_points = lax.slice_in_dim(points, 0, 1, axis=dimension)
    lower_dens = jnp.zeros_like(rising_dens)
    lower_points = jnp.zeros_like(rising_points)
    upper_dens = jnp.zeros_like(falling_dens)
    upper_points = jnp.zeros_like(falling_points)
    carried = (rising_dens, rising_points, falling_dens, falling_points)
    for bit_rank, global_bit in enumerate(range(dimension, total_bits, 3)):
        carried = flip(carried[0], carried[1], carried[2], carried[3], global_bit)
        got_lower = (carried[0], carried[1])
        got_upper = (carried[2], carried[3])
        bit_value = jnp.bitwise_and(jnp.right_shift(position, bit_rank), 1)
        below_bits = jnp.bitwise_and(position, (1 << bit_rank) - 1)
        from_lower = (bit_value == 1) & (below_bits == 0)
        from_upper = (bit_value == 0) & (below_bits == (1 << bit_rank) - 1)
        lower_dens = jnp.where(from_lower, got_lower[0], lower_dens)
        lower_points = jnp.where(from_lower, got_lower[1], lower_points)
        upper_dens = jnp.where(from_upper, got_upper[0], upper_dens)
        upper_points = jnp.where(from_upper, got_upper[1], upper_points)
    density = jnp.concatenate([lower_dens, density, upper_dens], axis=dimension)
    points = jnp.concatenate([lower_points, points, upper_points], axis=dimension)
    return (density, points)


def per_device(positions, charges, counts, up_inverse, down_inverse, inner_surface, outer_surface):
    point_flat, density = upward(positions, charges, counts, up_inverse, outer_surface)
    dens_grid = density.reshape(CX, CY, CZ, TERMS)
    point_grid = point_flat.reshape(CX, CY, CZ, 4, PTS)
    low_bits, mid_bits, high_bits = axis_bits()
    total_bits = low_bits + mid_bits + high_bits
    device = (lax.axis_index("gx") * lax.axis_size("gy") + lax.axis_index("gy")) * lax.axis_size(
        "gz"
    ) + lax.axis_index("gz")
    for dimension in range(3):
        dens_grid, point_grid = extend(dens_grid, point_grid, dimension, 2, device, total_bits)
    return potentials(
        counts,
        point_grid.reshape(EXT, 4, PTS),
        dens_grid.reshape(512, TERMS),
        down_inverse,
        inner_surface,
        outer_surface,
    )


def solution(mesh):
    in_specs = (
        P(("gx", "gy", "gz"), None, None),
        P(("gx", "gy", "gz"), None),
        P(("gx", "gy", "gz")),
        P(),
        P(),
        P(),
        P(),
    )
    out_specs = P(("gx", "gy", "gz"), None)
    return jax.shard_map(
        per_device, mesh=mesh, in_specs=in_specs, out_specs=out_specs, check_vma=False
    )
```

```python
from functools import partial

import jax
import jax.numpy as jnp
from jax import lax
from jax.experimental import pallas as pl
from jax.experimental.pallas import tpu as pltpu
from jax.sharding import PartitionSpec as P

CX = 4
CY = 4
CZ = 4
PTS = 128
TERMS = 64
LEAF = CX * CY * CZ
EXT = (CX + 2) * (CY + 2) * (CZ + 2)
FEATS = 32


SOFTEN = 0.0025
EXACT_DOTS = lax.Precision.HIGHEST


def iota(shape, dimension):
    return lax.broadcasted_iota(jnp.int32, shape, dimension)


def column(row):
    size = row.shape[1]
    eye = iota((size, size), 0) == iota((size, size), 1)
    return jnp.sum(jnp.where(eye, row, 0.0), axis=1, keepdims=True)


def rounded(value):
    return value.astype(jnp.bfloat16).astype(jnp.float32)


def three_parts(value):
    high = rounded(value)
    middle = rounded(value - high)
    low = rounded(value - high - middle)
    return high, middle, low


def upward_body(pos_ref, charge_ref, count_ref, up_ref, outer_ref, points_ref, dens_ref):
    lane = iota((1, PTS), 1)
    lanes = iota((TERMS, PTS), 1)
    spots = [jnp.broadcast_to(column(outer_ref[c : c + 1, :]), (TERMS, PTS)) for c in range(3)]

    def leaf(n, check):
        place = pos_ref[n]
        source = jnp.where(lane < count_ref[n], charge_ref[pl.ds(n, 1), :], 0.0)
        points_ref[n] = jnp.concatenate([place, source], axis=0)
        square = jnp.full((TERMS, PTS), SOFTEN, jnp.float32)
        for c in range(3):
            spread = spots[c] - place[c : c + 1, :]
            square = square + spread * spread
        total = jnp.sum(lax.rsqrt(square) * source, axis=1, keepdims=True)
        return jnp.where(lanes == n, total, check)

    check = lax.fori_loop(0, LEAF, leaf, jnp.zeros((TERMS, PTS), jnp.float32), unroll=4)
    dens = jnp.dot(
        up_ref[...], check, preferred_element_type=jnp.float32, precision=EXACT_DOTS
    )
    dens = jnp.transpose(jnp.concatenate([dens, dens], axis=0))
    for n in range(LEAF):
        dens_ref[n] = dens[n : n + 1]


def squares_of(points, shift_x, shift_y, shift_z, extra):
    row = iota((8, PTS), 0) % 4
    twice = jnp.concatenate([points, points], axis=0)
    place = twice + jnp.where(row == 0, shift_x, jnp.where(row == 1, shift_y, shift_z))
    square = place * place
    norm = square[0:1] + square[1:2] + square[2:3] + extra
    return jnp.where(row == 3, norm, place), row == 3, iota((8, PTS), 0) < 4


def source_features(points, shift_x, shift_y, shift_z):
    value, last, first = squares_of(points, shift_x, shift_y, shift_z, 0.0)
    high, middle, low = three_parts(value)
    scale = jnp.where(last, 1.0, -2.0)
    high_one = jnp.where(last, 1.0, -2.0 * high)
    middle_one = jnp.where(last, 1.0, -2.0 * middle)
    rows = [
        jnp.where(first, high * scale, middle * scale),
        jnp.where(first, low * scale, high_one),
        jnp.where(first, high_one, middle_one),
        jnp.zeros((8, PTS), jnp.float32),
    ]
    return jnp.concatenate(rows, axis=0).astype(jnp.bfloat16)


def target_features(points, shift_x, shift_y, shift_z):
    value, last, first = squares_of(points, shift_x, shift_y, shift_z, SOFTEN)
    high, middle, low = three_parts(value)
    high_one = jnp.where(last, 1.0, high)
    rows = [
        high_one,
        jnp.where(first, high_one, jnp.where(last, high, middle)),
        jnp.where(first, jnp.where(last, middle, low), jnp.where(last, low, middle)),
        jnp.zeros((8, PTS), jnp.float32),
    ]
    return jnp.transpose(jnp.concatenate(rows, axis=0)).astype(jnp.bfloat16)


def translate_part(dens_ref, inner_ref, down_ref, grouped, local):
    def clear(n, carry):
        grouped[pl.ds(n * 8, 8)] = jnp.zeros((8, 8, 2 * TERMS), jnp.float32)
        return carry

    lax.fori_loop(0, 64, clear, 0)

    def gather(n, carry):
        a_x = n // 6
        a_y = n % 6
        for a_z in range(6):
            to = (a_x + 1) * 64 + (a_y + 1) * 8 + a_z + 1
            for parent in range(8):
                cell_x = 2 * (parent // 4) + a_x
                cell_y = 2 * (parent // 2 % 2) + a_y
                cell_z = 2 * (parent % 2) + a_z
                cell = cell_x * 64 + cell_y * 8 + cell_z
                grouped[to, parent : parent + 1, :] = dens_ref[cell]
        return carry

    lax.fori_loop(0, 36, gather, 0)

    half = iota((8, 2 * TERMS), 1) < TERMS

    def split(n, carry):
        at = (n // 36 + 1) * 64 + (n // 6 % 6 + 1) * 8 + n % 6 + 1
        value = grouped[at]
        high = rounded(value)
        grouped[at] = jnp.where(half, high, value - high)
        return carry

    lax.fori_loop(0, 216, split, 0, unroll=4)
    first = iota((TERMS, 2 * TERMS), 1) < TERMS
    spread = []
    for c in range(3):
        row = inner_ref[c : c + 1, :]
        spread.append(jnp.concatenate([row, row], axis=1) - column(row))

    def shift_pair(n, total):
        shift_x = n // 7 - 3
        shift_y = n % 7 - 3
        d_x = spread[0] - shift_x.astype(jnp.float32)
        d_y = spread[1] - shift_y.astype(jnp.float32)
        plane = d_x * d_x + d_y * d_y + SOFTEN
        extent = jnp.maximum(jnp.abs(shift_x), jnp.abs(shift_y))
        lefts = []
        rights = []
        for shift_z in range(-3, 4):
            d_z = spread[2] - float(shift_z)
            weight = lax.rsqrt(plane + d_z * d_z)
            if abs(shift_z) < 2:
                weight = jnp.where(extent >= 2, weight, 0.0)
            upper = rounded(weight)
            right = jnp.where(first, upper, weight - upper).astype(jnp.bfloat16)
            rights += [right, right]
            pieces = []
            for parity in range(8):
                at = (
                    (shift_x + 3 + parity // 4) * 64
                    + (shift_y + 3 + parity // 2 % 2) * 8
                    + shift_z + 3 + parity % 2
                )
                pieces.append(grouped[at])
            lefts.append(jnp.concatenate(pieces, axis=0).astype(jnp.bfloat16))
        for at in range(0, 7, 2):
            left = jnp.concatenate(lefts[at : at + 2], axis=1)
            right = jnp.concatenate(rights[2 * at : 2 * at + 4], axis=0)
            total = total + jnp.dot(left, right, preferred_element_type=jnp.float32)
        return total

    total = lax.fori_loop(0, 49, shift_pair, jnp.zeros((LEAF, 2 * TERMS), jnp.float32))
    down = down_ref[...]
    down = jnp.concatenate([down, down], axis=1)
    down = jnp.concatenate([down, jnp.zeros_like(down)], axis=0)
    local[...] = lax.dot_general(
        total,
        down,
        (((1,), (1,)), ((), ())),
        preferred_element_type=jnp.float32,
        precision=EXACT_DOTS,
    )


def near_body(
    count_ref,
    points_ref,
    dens_ref,
    down_ref,
    inner_ref,
    outer_ref,
    out_ref,
    grouped,
    local,
    sources,
    targets,
    surface,
):
    translate_part(dens_ref, inner_ref, down_ref, grouped, local)
    surface[...] = jnp.zeros((4, PTS), jnp.float32)
    surface[0:3, 0:TERMS] = outer_ref[...]

    def middle(cell):
        return cell.astype(jnp.float32) - (CX // 2 + 1)

    def prepare(n, carry):
        e_x = n // ((CY + 2) * (CZ + 2))
        e_y = n // (CZ + 2) % (CY + 2)
        e_z = n % (CZ + 2)
        sources[n] = source_features(points_ref[n], middle(e_x), middle(e_y), middle(e_z))
        return carry

    lax.fori_loop(0, EXT, prepare, 0, unroll=4)

    def ext_index(n):
        return (n // (CY * CZ) + 1) * ((CY + 2) * (CZ + 2)) + (n // CZ % CY + 1) * (CZ + 2) + (
            n % CZ + 1
        )

    def prepare_own(n, carry):
        x = middle(n // (CY * CZ) + 1)
        y = middle(n // CZ % CY + 1)
        z = middle(n % CZ + 1)
        targets[n] = target_features(points_ref[ext_index(n)], x, y, z)
        sources[EXT + n] = source_features(surface[...], x, y, z)
        return carry

    lax.fori_loop(0, LEAF, prepare_own, 0, unroll=4)

    lane = iota((1, PTS), 1)

    def leaf(n, carry):
        base = ext_index(n)
        x = n // (CY * CZ)
        y = n // CZ % CY
        z = n % CZ
        parity = (x % 2) * 4 + (y % 2) * 2 + z % 2
        parent = (x // 2) * 4 + (y // 2) * 2 + z // 2
        count = count_ref[n]
        blocks = []
        for s_x in range(-1, 2):
            for s_y in range(-1, 2):
                for s_z in range(-1, 2):
                    blocks.append(base + s_x * ((CY + 2) * (CZ + 2)) + s_y * (CZ + 2) + s_z)

        def rows(size):
            left = targets[n, 0:size, :]
            eye = iota((size, PTS), 0) == iota((size, PTS), 1)
            total = jnp.zeros((size, PTS), jnp.float32)
            for at in range(0, 28, 2):
                right = []
                charge = []
                for b in (at, at + 1):
                    if b < 27:
                        right.append(sources[blocks[b]])
                        charge.append(points_ref[blocks[b], 3:4, :])
                    else:
                        right.append(sources[EXT + n])
                        charge.append(local[pl.ds(parity * 8 + parent, 1), :])
                square = jnp.dot(
                    left, jnp.concatenate(right, axis=1), preferred_element_type=jnp.float32
                )
                weight = lax.rsqrt(square)
                for k, b in enumerate((at, at + 1)):
                    part = weight[:, k * PTS : (k + 1) * PTS]
                    if b == 13:
                        part = jnp.where(eye, 0.0, part)
                    total = total + part * charge[k]
            sums = jnp.sum(total, axis=1, keepdims=True)
            flat = jnp.sum(jnp.where(eye, sums, 0.0), axis=0, keepdims=True)
            out_ref[pl.ds(n, 1), :] = jnp.where(lane < count, flat, 0.0)

        filled = (count + 31) // 32
        for k in range(1, 5):
            pl.when(filled == k)(partial(rows, 32 * k))
        return carry

    lax.fori_loop(0, LEAF, leaf, 0)


def whole():
    return pl.BlockSpec(memory_space=pltpu.VMEM)


def scalars():
    return pl.BlockSpec(memory_space=pltpu.SMEM)


def upward(positions, charges, counts, up_inverse, outer_surface):
    return pl.pallas_call(
        upward_body,
        out_shape=(
            jax.ShapeDtypeStruct((LEAF, 4, PTS), jnp.float32),
            jax.ShapeDtypeStruct((LEAF, 1, 2 * TERMS), jnp.float32),
        ),
        in_specs=[whole(), whole(), scalars(), whole(), whole()],
        out_specs=(whole(), whole()),
        name="upward",
    )(positions, charges, counts, up_inverse, outer_surface)


def potentials(counts, points, density, down_inverse, inner_surface, outer_surface):
    return pl.pallas_call(
        near_body,
        out_shape=jax.ShapeDtypeStruct((LEAF, PTS), jnp.float32),
        in_specs=[scalars()] + [whole()] * 5,
        out_specs=whole(),
        scratch_shapes=[
            pltpu.VMEM((512, 8, 2 * TERMS), jnp.float32),
            pltpu.VMEM((LEAF, 2 * TERMS), jnp.float32),
            pltpu.VMEM((EXT + LEAF, FEATS, PTS), jnp.bfloat16),
            pltpu.VMEM((LEAF, PTS, FEATS), jnp.bfloat16),
            pltpu.VMEM((4, PTS), jnp.float32),
        ],
        compiler_params=pltpu.CompilerParams(vmem_limit_bytes=50 * 2**20),
        name="potentials",
    )(counts, points, density, down_inverse, inner_surface, outer_surface)


def axis_bits():
    low_bits = lax.axis_size("gz").bit_length() - 1
    mid_bits = lax.axis_size("gy").bit_length() - 1
    high_bits = lax.axis_size("gx").bit_length() - 1
    return (low_bits, mid_bits, high_bits)


SIDES = [
    (x, y, z)
    for x in (-1, 0, 1)
    for y in (-1, 0, 1)
    for z in (-1, 0, 1)
    if (x, y, z) != (0, 0, 0)
]


def rim(side, size, layers):
    if side > 0:
        return pl.ds(size - layers, layers), pl.ds(0, layers)
    if side < 0:
        return pl.ds(0, layers), pl.ds(size + layers, layers)
    return pl.ds(0, size), pl.ds(layers, size)


def exchange_body(points_ref, dens_ref, wide_points, wide_dens, send_sem, recv_sem):
    low_bits, mid_bits, high_bits = axis_bits()
    total_bits = low_bits + mid_bits + high_bits
    device = (
        lax.axis_index("gx") * 2**mid_bits + lax.axis_index("gy")
    ) * 2**low_bits + lax.axis_index("gz")
    place = []
    extent = []
    for c in range(3):
        bits = list(range(c, total_bits, 3))
        place.append(sum((device // 2**bit % 2) * 2**rank for rank, bit in enumerate(bits)))
        extent.append(2 ** len(bits))

    def there(side):
        inside = jnp.bool_(True)
        for c in range(3):
            if side[c] > 0:
                inside = inside & (place[c] < extent[c] - 1)
            if side[c] < 0:
                inside = inside & (place[c] > 0)
        return inside

    def coordinates(side):
        other = 0
        for c in range(3):
            moved = place[c] + side[c]
            for rank, bit in enumerate(range(c, total_bits, 3)):
                other = other + (moved // 2**rank % 2) * 2**bit
        return (
            other // 2 ** (low_bits + mid_bits),
            other // 2**low_bits % 2**mid_bits,
            other % 2**low_bits,
        )

    def copies(at):
        side = SIDES[at]
        sizes = (CX, CY, CZ)
        result = []
        for kind, (own, wide, layers) in enumerate(
            ((dens_ref, wide_dens, 2), (points_ref, wide_points, 1))
        ):
            source, target = zip(*(rim(side[c], sizes[c], layers) for c in range(3)))
            result.append(
                pltpu.make_async_remote_copy(
                    src_ref=own.at[source],
                    dst_ref=wide.at[target],
                    send_sem=send_sem.at[kind, at],
                    recv_sem=recv_sem.at[kind, at],
                    device_id=coordinates(side),
                    device_id_type=pl.DeviceIdType.MESH,
                )
            )
        return result

    def clear(n, carry):
        wide_points[n] = jnp.zeros(wide_points.shape[1:], jnp.float32)
        return carry

    def clear_dens(n, carry):
        wide_dens[n] = jnp.zeros(wide_dens.shape[1:], jnp.float32)
        return carry

    lax.fori_loop(0, CX + 2, clear, 0)
    lax.fori_loop(0, CX + 4, clear_dens, 0)
    barrier = pltpu.get_barrier_semaphore()
    met = jnp.int32(0)
    for side in SIDES:
        inside = there(side)
        met = met + jnp.where(inside, 1, 0)

        @pl.when(inside)
        def _(side=side):
            pl.semaphore_signal(
                barrier,
                inc=1,
                device_id=coordinates(side),
                device_id_type=pl.DeviceIdType.MESH,
            )

    pl.semaphore_wait(barrier, met)
    order = sorted(range(len(SIDES)), key=lambda at: sum(map(abs, SIDES[at])))
    for at in order:

        @pl.when(there(SIDES[at]))
        def _(at=at):
            for copy in copies(at):
                copy.start()

    for x in range(CX):
        wide_points[x + 1, 1 : CY + 1, 1 : CZ + 1] = points_ref[x]
        wide_dens[x + 2, 2 : CY + 2, 2 : CZ + 2] = dens_ref[x]
    for at in order:

        @pl.when(there(SIDES[at]))
        def _(at=at):
            for copy in copies(at):
                copy.wait_send()

        @pl.when(there(tuple(-c for c in SIDES[at])))
        def _(at=at):
            for copy in copies(at):
                copy.wait_recv()


def exchange(points, density):
    return pl.pallas_call(
        exchange_body,
        out_shape=(
            jax.ShapeDtypeStruct((CX + 2, CY + 2, CZ + 2, 4, PTS), jnp.float32),
            jax.ShapeDtypeStruct((CX + 4, CY + 4, CZ + 4, 1, 2 * TERMS), jnp.float32),
        ),
        in_specs=[whole(), whole()],
        out_specs=(whole(), whole()),
        scratch_shapes=[
            pltpu.SemaphoreType.DMA((2, len(SIDES))),
            pltpu.SemaphoreType.DMA((2, len(SIDES))),
        ],
        compiler_params=pltpu.CompilerParams(collective_id=0, has_side_effects=True),
        name="exchange",
    )(points, density)


def per_device(positions, charges, counts, up_inverse, down_inverse, inner_surface, outer_surface):
    point_flat, density = upward(positions, charges, counts, up_inverse, outer_surface)
    point_grid, dens_grid = exchange(
        point_flat.reshape(CX, CY, CZ, 4, PTS), density.reshape(CX, CY, CZ, 1, 2 * TERMS)
    )
    return potentials(
        counts,
        point_grid.reshape(EXT, 4, PTS),
        dens_grid.reshape(512, 1, 2 * TERMS),
        down_inverse,
        inner_surface,
        outer_surface,
    )


def solution(mesh):
    in_specs = (
        P(("gx", "gy", "gz"), None, None),
        P(("gx", "gy", "gz"), None),
        P(("gx", "gy", "gz")),
        P(),
        P(),
        P(),
        P(),
    )
    out_specs = P(("gx", "gy", "gz"), None)
    return jax.shard_map(
        per_device, mesh=mesh, in_specs=in_specs, out_specs=out_specs, check_vma=False
    )
```

```python
from functools import partial

import jax
import jax.numpy as jnp
from jax import lax
from jax.experimental import pallas as pl
from jax.experimental.pallas import tpu as pltpu
from jax.sharding import PartitionSpec as P

CX = 4
CY = 4
CZ = 4
PTS = 128
TERMS = 64
LEAF = CX * CY * CZ
EXT = (CX + 2) * (CY + 2) * (CZ + 2)
FEATS = 32
LINE = 4


SOFTEN = 0.0025
EXACT_DOTS = lax.Precision.HIGHEST


def iota(shape, dimension):
    return lax.broadcasted_iota(jnp.int32, shape, dimension)


def column(row):
    size = row.shape[1]
    eye = iota((size, size), 0) == iota((size, size), 1)
    return jnp.sum(jnp.where(eye, row, 0.0), axis=1, keepdims=True)


def over_plane(size_x, size_y, body, start, unroll=1):
    def line(x, carry):
        return lax.fori_loop(0, size_y, lambda y, held: body(x, y, held), carry, unroll=unroll)

    return lax.fori_loop(0, size_x, line, start)


def rounded(value):
    return value.astype(jnp.bfloat16).astype(jnp.float32)


def three_parts(value):
    high = rounded(value)
    middle = rounded(value - high)
    low = rounded(value - high - middle)
    return high, middle, low


def upward_body(pos_ref, charge_ref, count_ref, up_ref, outer_ref, points_ref, dens_ref):
    lane = iota((1, PTS), 1)
    lanes = iota((TERMS, PTS), 1)
    spots = [jnp.broadcast_to(column(outer_ref[c : c + 1, :]), (TERMS, PTS)) for c in range(3)]

    def leaf(n, check):
        place = pos_ref[n]
        source = jnp.where(lane < count_ref[n], charge_ref[pl.ds(n, 1), :], 0.0)
        points_ref[n] = jnp.concatenate([place, source], axis=0)
        square = jnp.full((TERMS, PTS), SOFTEN, jnp.float32)
        for c in range(3):
            spread = spots[c] - place[c : c + 1, :]
            square = square + spread * spread
        total = jnp.sum(lax.rsqrt(square) * source, axis=1, keepdims=True)
        return jnp.where(lanes == n, total, check)

    check = lax.fori_loop(0, LEAF, leaf, jnp.zeros((TERMS, PTS), jnp.float32), unroll=4)
    dens = jnp.dot(
        up_ref[...], check, preferred_element_type=jnp.float32, precision=EXACT_DOTS
    )
    dens = jnp.transpose(jnp.concatenate([dens, dens], axis=0))
    for n in range(LEAF):
        dens_ref[n] = dens[n : n + 1]


def squares_of(points, shift_x, shift_y, shift_z, extra):
    row = iota((8, PTS), 0) % 4
    twice = jnp.concatenate([points, points], axis=0)
    place = twice + jnp.where(row == 0, shift_x, jnp.where(row == 1, shift_y, shift_z))
    square = place * place
    norm = square[0:1] + square[1:2] + square[2:3] + extra
    return jnp.where(row == 3, norm, place), row == 3, iota((8, PTS), 0) < 4


def source_features(points, shift_x, shift_y, shift_z):
    value, last, first = squares_of(points, shift_x, shift_y, shift_z, 0.0)
    high, middle, low = three_parts(value)
    scale = jnp.where(last, 1.0, -2.0)
    high_one = jnp.where(last, 1.0, -2.0 * high)
    middle_one = jnp.where(last, 1.0, -2.0 * middle)
    rows = [
        jnp.where(first, high * scale, middle * scale),
        jnp.where(first, low * scale, high_one),
        jnp.where(first, high_one, middle_one),
        jnp.zeros((8, PTS), jnp.float32),
    ]
    return jnp.concatenate(rows, axis=0).astype(jnp.bfloat16)


def target_features(points, shift_x, shift_y, shift_z):
    value, last, first = squares_of(points, shift_x, shift_y, shift_z, SOFTEN)
    high, middle, low = three_parts(value)
    high_one = jnp.where(last, 1.0, high)
    rows = [
        high_one,
        jnp.where(first, high_one, jnp.where(last, high, middle)),
        jnp.where(first, jnp.where(last, middle, low), jnp.where(last, low, middle)),
        jnp.zeros((8, PTS), jnp.float32),
    ]
    return jnp.transpose(jnp.concatenate(rows, axis=0)).astype(jnp.bfloat16)


def translate_part(dens_ref, inner_ref, down_ref, grouped, local):
    def clear(n, carry):
        grouped[pl.ds(n * 8, 8)] = jnp.zeros((8, 8, 2 * TERMS), jnp.float32)
        return carry

    lax.fori_loop(0, 64, clear, 0)

    def gather(a_x, a_y, carry):
        for a_z in range(6):
            to = (a_x + 1) * 64 + (a_y + 1) * 8 + a_z + 1
            for parent in range(8):
                cell_x = 2 * (parent // 4) + a_x
                cell_y = 2 * (parent // 2 % 2) + a_y
                cell_z = 2 * (parent % 2) + a_z
                cell = cell_x * 64 + cell_y * 8 + cell_z
                grouped[to, parent : parent + 1, :] = dens_ref[cell]
        return carry

    over_plane(6, 6, gather, 0, 6)

    half = iota((8, 2 * TERMS), 1) < TERMS

    def split(a_x, a_y, carry):
        for a_z in range(6):
            at = (a_x + 1) * 64 + (a_y + 1) * 8 + a_z + 1
            value = grouped[at]
            high = rounded(value)
            grouped[at] = jnp.where(half, high, value - high)
        return carry

    over_plane(6, 6, split, 0, 6)
    first = iota((TERMS, 2 * TERMS), 1) < TERMS
    spread = []
    for c in range(3):
        row = inner_ref[c : c + 1, :]
        spread.append(jnp.concatenate([row, row], axis=1) - column(row))

    def shift_pair(n_x, n_y, total):
        shift_x = n_x - 3
        shift_y = n_y - 3
        d_x = spread[0] - shift_x.astype(jnp.float32)
        d_y = spread[1] - shift_y.astype(jnp.float32)
        plane = d_x * d_x + d_y * d_y + SOFTEN
        extent = jnp.maximum(jnp.abs(shift_x), jnp.abs(shift_y))
        lefts = []
        rights = []
        for shift_z in range(-3, 4):
            d_z = spread[2] - float(shift_z)
            weight = lax.rsqrt(plane + d_z * d_z)
            if abs(shift_z) < 2:
                weight = jnp.where(extent >= 2, weight, 0.0)
            upper = rounded(weight)
            right = jnp.where(first, upper, weight - upper).astype(jnp.bfloat16)
            rights += [right, right]
            pieces = []
            for parity in range(8):
                at = (
                    (shift_x + 3 + parity // 4) * 64
                    + (shift_y + 3 + parity // 2 % 2) * 8
                    + shift_z + 3 + parity % 2
                )
                pieces.append(grouped[at])
            lefts.append(jnp.concatenate(pieces, axis=0).astype(jnp.bfloat16))
        for at in range(0, 7, 2):
            left = jnp.concatenate(lefts[at : at + 2], axis=1)
            right = jnp.concatenate(rights[2 * at : 2 * at + 4], axis=0)
            total = total + jnp.dot(left, right, preferred_element_type=jnp.float32)
        return total

    total = over_plane(7, 7, shift_pair, jnp.zeros((LEAF, 2 * TERMS), jnp.float32), 7)
    down = down_ref[...]
    down = jnp.concatenate([down, down], axis=1)
    down = jnp.concatenate([down, jnp.zeros_like(down)], axis=0)
    local[...] = lax.dot_general(
        total,
        down,
        (((1,), (1,)), ((), ())),
        preferred_element_type=jnp.float32,
        precision=EXACT_DOTS,
    )


def near_body(
    count_ref,
    points_ref,
    dens_ref,
    down_ref,
    inner_ref,
    outer_ref,
    out_ref,
    grouped,
    local,
    sources,
    targets,
    surface,
):
    translate_part(dens_ref, inner_ref, down_ref, grouped, local)
    surface[...] = jnp.zeros((4, PTS), jnp.float32)
    surface[0:3, 0:TERMS] = outer_ref[...]

    def middle(cell):
        return jnp.float32(cell) - (CX // 2 + 1) if isinstance(cell, int) else (
            cell.astype(jnp.float32) - (CX // 2 + 1)
        )

    def prepare(e_x, e_y, carry):
        for e_z in range(CZ + 2):
            n = (e_x * (CY + 2) + e_y) * (CZ + 2) + e_z
            sources[n] = source_features(points_ref[n], middle(e_x), middle(e_y), middle(e_z))
        return carry

    over_plane(CX + 2, CY + 2, prepare, 0, CY + 2)

    def ext_index(x, y, z):
        return ((x + 1) * (CY + 2) + y + 1) * (CZ + 2) + z + 1

    def prepare_own(x, y, carry):
        for z in range(CZ):
            n = (x * CY + y) * CZ + z
            place = (middle(x + 1), middle(y + 1), middle(z + 1))
            targets[n] = target_features(points_ref[ext_index(x, y, z)], *place)
            sources[EXT + n] = source_features(surface[...], *place)
        return carry

    over_plane(CX, CY, prepare_own, 0, CY)

    lane = iota((1, PTS), 1)

    def leaf(x, y, z):
        n = (x * CY + y) * CZ + z
        base = ext_index(x, y, z)
        parity = (x & 1) * 4 + (y & 1) * 2 + (z & 1)
        parent = (x >> 1) * 4 + (y >> 1) * 2 + (z >> 1)
        count = count_ref[n]
        blocks = []
        for s_x in range(-1, 2):
            for s_y in range(-1, 2):
                for s_z in range(-1, 2):
                    blocks.append(base + s_x * ((CY + 2) * (CZ + 2)) + s_y * (CZ + 2) + s_z)

        def rows(size):
            left = targets[n, 0:size, :]
            eye = iota((size, PTS), 0) == iota((size, PTS), 1)
            total = jnp.zeros((size, PTS), jnp.float32)
            for at in range(0, 28, 2):
                right = []
                charge = []
                for b in (at, at + 1):
                    if b < 27:
                        right.append(sources[blocks[b]])
                        charge.append(points_ref[blocks[b], 3:4, :])
                    else:
                        right.append(sources[EXT + n])
                        charge.append(local[pl.ds(parity * 8 + parent, 1), :])
                square = jnp.dot(
                    left, jnp.concatenate(right, axis=1), preferred_element_type=jnp.float32
                )
                weight = lax.rsqrt(square)
                for k, b in enumerate((at, at + 1)):
                    part = weight[:, k * PTS : (k + 1) * PTS]
                    if b == 13:
                        part = jnp.where(eye, 0.0, part)
                    total = total + part * charge[k]
            sums = jnp.sum(total, axis=1, keepdims=True)
            flat = jnp.sum(jnp.where(eye, sums, 0.0), axis=0, keepdims=True)
            out_ref[pl.ds(n, 1), :] = jnp.where(lane < count, flat, 0.0)

        return (count + 31) >> 5, rows

    def leaf_group(x, y, z):
        group = [leaf(x, y, z + k) for k in range(LINE)]
        most = group[0][0]
        for filled, _ in group[1:]:
            most = jnp.maximum(most, filled)

        def together(size):
            for _, rows in group:
                rows(size)

        for k in range(1, 5):
            pl.when(most == k)(partial(together, 32 * k))

    def leaf_line(x, y, carry):
        if LINE == CZ:
            leaf_group(x, y, 0)
        else:
            for z in range(0, CZ, LINE):
                leaf_group(x, y, z)
        return carry

    over_plane(CX, CY, leaf_line, 0)


def whole():
    return pl.BlockSpec(memory_space=pltpu.VMEM)


def scalars():
    return pl.BlockSpec(memory_space=pltpu.SMEM)


def upward(positions, charges, counts, up_inverse, outer_surface):
    return pl.pallas_call(
        upward_body,
        out_shape=(
            jax.ShapeDtypeStruct((LEAF, 4, PTS), jnp.float32),
            jax.ShapeDtypeStruct((LEAF, 1, 2 * TERMS), jnp.float32),
        ),
        in_specs=[whole(), whole(), scalars(), whole(), whole()],
        out_specs=(whole(), whole()),
        name="upward",
    )(positions, charges, counts, up_inverse, outer_surface)


def potentials(counts, points, density, down_inverse, inner_surface, outer_surface):
    return pl.pallas_call(
        near_body,
        out_shape=jax.ShapeDtypeStruct((LEAF, PTS), jnp.float32),
        in_specs=[scalars()] + [whole()] * 5,
        out_specs=whole(),
        scratch_shapes=[
            pltpu.VMEM((512, 8, 2 * TERMS), jnp.float32),
            pltpu.VMEM((LEAF, 2 * TERMS), jnp.float32),
            pltpu.VMEM((EXT + LEAF, FEATS, PTS), jnp.bfloat16),
            pltpu.VMEM((LEAF, PTS, FEATS), jnp.bfloat16),
            pltpu.VMEM((4, PTS), jnp.float32),
        ],
        compiler_params=pltpu.CompilerParams(vmem_limit_bytes=50 * 2**20),
        name="potentials",
    )(counts, points, density, down_inverse, inner_surface, outer_surface)


def axis_bits():
    low_bits = lax.axis_size("gz").bit_length() - 1
    mid_bits = lax.axis_size("gy").bit_length() - 1
    high_bits = lax.axis_size("gx").bit_length() - 1
    return (low_bits, mid_bits, high_bits)


SIDES = [
    (x, y, z)
    for x in (-1, 0, 1)
    for y in (-1, 0, 1)
    for z in (-1, 0, 1)
    if (x, y, z) != (0, 0, 0)
]


def rim(side, size, layers):
    if side > 0:
        return pl.ds(size - layers, layers), pl.ds(0, layers)
    if side < 0:
        return pl.ds(0, layers), pl.ds(size + layers, layers)
    return pl.ds(0, size), pl.ds(layers, size)


def exchange_body(points_ref, dens_ref, wide_points, wide_dens, send_sem, recv_sem):
    low_bits, mid_bits, high_bits = axis_bits()
    total_bits = low_bits + mid_bits + high_bits
    device = (
        lax.axis_index("gx") * 2**mid_bits + lax.axis_index("gy")
    ) * 2**low_bits + lax.axis_index("gz")
    place = []
    extent = []
    for c in range(3):
        bits = list(range(c, total_bits, 3))
        place.append(sum((device // 2**bit % 2) * 2**rank for rank, bit in enumerate(bits)))
        extent.append(2 ** len(bits))

    def there(side):
        inside = jnp.bool_(True)
        for c in range(3):
            if side[c] > 0:
                inside = inside & (place[c] < extent[c] - 1)
            if side[c] < 0:
                inside = inside & (place[c] > 0)
        return inside

    def coordinates(side):
        other = 0
        for c in range(3):
            moved = place[c] + side[c]
            for rank, bit in enumerate(range(c, total_bits, 3)):
                other = other + (moved // 2**rank % 2) * 2**bit
        return (
            other // 2 ** (low_bits + mid_bits),
            other // 2**low_bits % 2**mid_bits,
            other % 2**low_bits,
        )

    def copies(at):
        side = SIDES[at]
        sizes = (CX, CY, CZ)
        result = []
        for kind, (own, wide, layers) in enumerate(
            ((dens_ref, wide_dens, 2), (points_ref, wide_points, 1))
        ):
            source, target = zip(*(rim(side[c], sizes[c], layers) for c in range(3)))
            result.append(
                pltpu.make_async_remote_copy(
                    src_ref=own.at[source],
                    dst_ref=wide.at[target],
                    send_sem=send_sem.at[kind, at],
                    recv_sem=recv_sem.at[kind, at],
                    device_id=coordinates(side),
                    device_id_type=pl.DeviceIdType.MESH,
                )
            )
        return result

    def clear(n, carry):
        wide_points[n] = jnp.zeros(wide_points.shape[1:], jnp.float32)
        return carry

    def clear_dens(n, carry):
        wide_dens[n] = jnp.zeros(wide_dens.shape[1:], jnp.float32)
        return carry

    lax.fori_loop(0, CX + 2, clear, 0)
    lax.fori_loop(0, CX + 4, clear_dens, 0)
    barrier = pltpu.get_barrier_semaphore()
    met = jnp.int32(0)
    for side in SIDES:
        inside = there(side)
        met = met + jnp.where(inside, 1, 0)

        @pl.when(inside)
        def _(side=side):
            pl.semaphore_signal(
                barrier,
                inc=1,
                device_id=coordinates(side),
                device_id_type=pl.DeviceIdType.MESH,
            )

    pl.semaphore_wait(barrier, met)
    order = sorted(range(len(SIDES)), key=lambda at: sum(map(abs, SIDES[at])))
    for at in order:

        @pl.when(there(SIDES[at]))
        def _(at=at):
            for copy in copies(at):
                copy.start()

    for x in range(CX):
        wide_points[x + 1, 1 : CY + 1, 1 : CZ + 1] = points_ref[x]
        wide_dens[x + 2, 2 : CY + 2, 2 : CZ + 2] = dens_ref[x]
    for at in order:

        @pl.when(there(SIDES[at]))
        def _(at=at):
            for copy in copies(at):
                copy.wait_send()

        @pl.when(there(tuple(-c for c in SIDES[at])))
        def _(at=at):
            for copy in copies(at):
                copy.wait_recv()


def exchange(points, density):
    return pl.pallas_call(
        exchange_body,
        out_shape=(
            jax.ShapeDtypeStruct((CX + 2, CY + 2, CZ + 2, 4, PTS), jnp.float32),
            jax.ShapeDtypeStruct((CX + 4, CY + 4, CZ + 4, 1, 2 * TERMS), jnp.float32),
        ),
        in_specs=[whole(), whole()],
        out_specs=(whole(), whole()),
        scratch_shapes=[
            pltpu.SemaphoreType.DMA((2, len(SIDES))),
            pltpu.SemaphoreType.DMA((2, len(SIDES))),
        ],
        compiler_params=pltpu.CompilerParams(collective_id=0, has_side_effects=True),
        name="exchange",
    )(points, density)


def per_device(positions, charges, counts, up_inverse, down_inverse, inner_surface, outer_surface):
    point_flat, density = upward(positions, charges, counts, up_inverse, outer_surface)
    point_grid, dens_grid = exchange(
        point_flat.reshape(CX, CY, CZ, 4, PTS), density.reshape(CX, CY, CZ, 1, 2 * TERMS)
    )
    return potentials(
        counts,
        point_grid.reshape(EXT, 4, PTS),
        dens_grid.reshape(512, 1, 2 * TERMS),
        down_inverse,
        inner_surface,
        outer_surface,
    )


def solution(mesh):
    in_specs = (
        P(("gx", "gy", "gz"), None, None),
        P(("gx", "gy", "gz"), None),
        P(("gx", "gy", "gz")),
        P(),
        P(),
        P(),
        P(),
    )
    out_specs = P(("gx", "gy", "gz"), None)
    return jax.shard_map(
        per_device, mesh=mesh, in_specs=in_specs, out_specs=out_specs, check_vma=False
    )
```
